256 devices in a mesh: row: 16 (over z_hi, y), col: 16 (over x, z_lo, core).
Axes of the slice: x: 4, y: 4, z: 8 (z_hi: 4, z_lo: 2; z = z_hi * 2 + z_lo), core: 2. Of those that a mesh axis runs over, the one named last changes fastest.
Arguments:
- positions: float32 [3, 32768], P(None, ('row', 'col')), may hold values from 0 to 1
- radii: float32 [32768], P(('row', 'col')), may hold values from 0.5 to 2
- right_side: float32 [32768, 256], P(('row', 'col')), may hold values from -60 to 60, as said below
Outputs:
- solution: float32 [32768, 256], P(('row', 'col'))
- residual: float32 [32768, 256], P(('row', 'col'))
The draws below stay inside these ranges and needn't reach their ends.
Inputs may be any that keep to these rules, and one draw needn't show every extreme that they name: `right_side`: real values of varying scale.
All inputs are finite; a program needn't handle non-finite values.
Results may differ from the reference program's by a relative error of at most 0.0003.
Values sent between devices are 32-bit elements; how exact they have to be, the bound alone decides.
A program may use at most 64 MiB of HBM per device.

```python
import math
import jax
import jax.numpy as jnp
from jax import lax

NRHS = 256
ITERS = 2
NP = 32768


def draw_right_side(key, part):
    key_rows, key_cols, key_base = jax.random.split(key, 3)
    growth_ramp = jnp.exp(jnp.log(3.0) * jnp.arange(NP, dtype=jnp.float32) / NP)
    row_factor = jnp.exp(jax.random.uniform(key_rows, (NP, 1), minval=0.0, maxval=jnp.log(10.0)))
    col_factor = jnp.exp(jax.random.uniform(key_cols, (1, NRHS), minval=jnp.log(0.5), maxval=jnp.log(2.0)))
    base_draw = jnp.clip(jax.random.normal(key_base, (NP, NRHS)), -6.0, 6.0)
    scaled = base_draw * growth_ramp[:, None] * row_factor * col_factor / 6.0
    return scaled.astype(jnp.float32)


def block_levels(stream_key, extent, pieces, least, top_value):
    factor_of = 1.0
    for dim, shards_of in pieces:
        heights = jax.random.uniform(jax.random.fold_in(jax.random.fold_in(stream_key, 6), dim), (shards_of,), jnp.float32, least / len(pieces), top_value / len(pieces))
        factor_of = factor_of * jnp.repeat(jnp.exp(heights), extent[dim] // shards_of).reshape((-1,) + (1,) * (len(extent) - 1 - dim))
    return factor_of


def setup_inputs(seed: int = 0) -> dict:
    streams_of = jax.random.split(jax.random.key(seed), 4)
    return {
        "positions": jnp.clip(1.0 * jax.random.uniform(streams_of[0], (3, NP), jnp.float32) ** block_levels(streams_of[0], (3, NP), ((1, 256),), -0.2, 0.2), 0.0, 1.0),
        "radii": jnp.clip(jnp.exp(math.log(2.0) - 1.3862944 * jax.random.uniform(streams_of[1], (NP,), jnp.float32) ** block_levels(streams_of[1], (NP,), ((0, 256),), -0.2, 0.2)), 0.5, 2.0),
        "right_side": draw_right_side(jax.random.fold_in(streams_of[3], 71), 0),
    }


def kernel_product(row_points, col_points, values, kernel_scale, softening, limit):
    row_count = row_points.shape[1]
    col_count = col_points.shape[1]
    blocks = max(1, row_count * col_count // limit)
    while row_count % blocks:
        blocks = blocks - 1
    block_size = row_count // blocks
    grouped = row_points.reshape(3, blocks, block_size).transpose(1, 0, 2)

    def apply_block(row_block):
        first = row_block[0][:, None] - col_points[0][None, :]
        second = row_block[1][:, None] - col_points[1][None, :]
        third = row_block[2][:, None] - col_points[2][None, :]
        squared = first * first + second * second + third * third
        weights = lax.rsqrt(squared + softening) * kernel_scale
        return jnp.dot(weights, values, preferred_element_type=jnp.float32, precision=lax.Precision.HIGHEST)
    return lax.map(apply_block, grouped).reshape(row_count, values.shape[1])

def constants(total):
    kernel_scale = float(total) ** (-0.5)
    spacing = 0.25 * float(total) ** (-1.0 / 3.0)
    return (kernel_scale, spacing * spacing)

def reference(positions, radii, right_side):
    kernel_scale, softening = constants(NP)

    def operator(vector):
        coupled = kernel_product(positions, positions, vector, kernel_scale, softening, 1 << 22)
        return vector / radii[:, None] + coupled
    solution = jnp.zeros_like(right_side)
    residual = right_side
    direction = right_side
    norm_now = lax.optimization_barrier(jnp.sum(residual * residual, axis=0))
    for iteration in range(ITERS):
        image_vec = operator(direction)
        step_size = norm_now / lax.optimization_barrier(jnp.sum(direction * image_vec, axis=0))
        solution = solution + step_size * direction
        residual = residual - step_size * image_vec
        if iteration + 1 < ITERS:
            norm_next = lax.optimization_barrier(jnp.sum(residual * residual, axis=0))
            direction = residual + norm_next / norm_now * direction
            norm_now = norm_next
    return (solution, residual)
```

```python
import functools

import jax
import jax.numpy as jnp
from jax import lax
from jax.experimental import pallas as pl
from jax.experimental.pallas import tpu as pltpu
from jax.sharding import PartitionSpec as P

MESH = pl.DeviceIdType.MESH
B = 128
R = 256
NX, NY, NZ = 4, 4, 8
PLANE = NX * NY
LINE = NZ * 2
HALF = B // 2
SUB = 4
SR = B // SUB
F32 = jnp.float32
BF16 = jnp.bfloat16


def constants(total):
    kernel_scale = float(total) ** (-0.5)
    spacing = 0.25 * float(total) ** (-1.0 / 3.0)
    return (kernel_scale, spacing * spacing)


def kernel(
    kernel_scale, softening,
    pos_ref, rad_ref, b_ref, sol_ref, res_ref,
    khi, klo, gath, vhi, vlo, part, sib, ring, xb, ppos, lpos, own_pos, w1, w2, r1, ar_src, ar_plane, ar_line,
    pos_send, pos_recv, g_send, g_recv, s_send, s_recv, r_send, r_recv, ar_send, ar_recv,
):
    row, col = lax.axis_index("row"), lax.axis_index("col")
    x, y = col // 4, lax.rem(row, 4)
    z, k = (row // 4) * 2 + lax.rem(col // 2, 2), lax.rem(col, 2)

    def device(xx, yy, zz, kk):
        return {"row": (zz // 2) * 4 + yy, "col": xx * 4 + lax.rem(zz, 2) * 2 + kk}

    def at_x(d):
        return lax.rem(x + d, NX)

    def at_y(d):
        return lax.rem(y + d, NY)

    def at_z(d):
        return lax.rem(z + d, NZ)

    def send(src, dst, ssem, rsem, dev):
        pltpu.make_async_remote_copy(
            src_ref=src, dst_ref=dst, send_sem=ssem, recv_sem=rsem, device_id=dev, device_id_type=MESH
        ).start()

    def wait(ref, sem):
        pltpu.make_async_copy(ref, ref, sem).wait()

    plane_peers = [device(at_x(dx), at_y(dy), z, k) for dx in range(NX) for dy in range(NY) if dx or dy]
    line_peers = [
        device(x, y, at_z(dz), lax.rem(k + dk, 2)) for dz in range(NZ) for dk in range(2) if dz or dk
    ]
    sibling = device(x, y, z, 1 - k)
    slot = x * NY + y
    line_slot = z * 2 + k

    barrier = pltpu.get_barrier_semaphore()
    for peer in plane_peers + line_peers:
        pl.semaphore_signal(barrier, 1, device_id=peer, device_id_type=MESH)
    own_pos[...] = jnp.zeros_like(own_pos)
    own_pos[0:3, :] = pos_ref[...]
    own_pos[3:4, :] = rad_ref[...]
    pl.semaphore_wait(barrier, len(plane_peers) + len(line_peers))

    def half_rows(h):
        return pl.ds(h * HALF, HALF)

    def gather_start(m, src, h):
        for d in (2, 1, 3):
            first = device(at_x(d), y, z, k) if h == 0 else device(x, at_y(d), z, k)
            send(src.at[half_rows(h)], gath.at[m, slot, half_rows(h)], g_send.at[m], g_recv.at[m, h, slot], first)
        for d in (2, 1, 3):
            second = device(x, at_y(d), z, k) if h == 0 else device(at_x(d), y, z, k)
            send(src.at[half_rows(h)], gath.at[m, slot, half_rows(h)], g_send.at[m], g_recv.at[m, h, slot], second)

    def gather_forward(m):
        for o in (1, 3, 2):
            for h in range(2):
                s = at_x(o) * NY + y if h == 0 else x * NY + at_y(o)
                piece = gath.at[m, s, half_rows(h)]
                wait(piece, g_recv.at[m, h, s])
                for d in (2, 1, 3):
                    second = device(x, at_y(d), z, k) if h == 0 else device(at_x(d), y, z, k)
                    send(piece, piece, g_send.at[m], g_recv.at[m, h, s], second)

    def gather_finish(m):
        for dx in range(NX):
            for dy in range(NY):
                s = at_x(dx) * NY + at_y(dy)
                for h in range(2):
                    if (dy if h == 0 else dx) != 0:
                        wait(gath.at[m, s, half_rows(h)], g_recv.at[m, h, s])

    def sum_start(i):
        ar_plane[i, slot] = ar_src[i]
        for peer in plane_peers:
            send(ar_src.at[i], ar_plane.at[i, slot], ar_send.at[i, 0], ar_recv.at[i, 0], peer)

    def sum_middle(i):
        wait(ar_plane.at[i, 0 : PLANE - 1], ar_send.at[i, 0])
        wait(ar_plane.at[i, 0 : PLANE - 1], ar_recv.at[i, 0])
        total = ar_plane[i, 0]
        for s in range(1, PLANE):
            total = total + ar_plane[i, s]
        ar_src[i] = total
        ar_line[i, line_slot] = total
        for peer in line_peers:
            send(ar_src.at[i], ar_line.at[i, line_slot], ar_send.at[i, 1], ar_recv.at[i, 1], peer)

    def sum_finish(i):
        wait(ar_line.at[i, 0 : LINE - 1], ar_recv.at[i, 1])
        total = ar_line[i, 0]
        for s in range(1, LINE):
            total = total + ar_line[i, s]
        return total

    for peer in plane_peers:
        send(own_pos, ppos.at[slot], pos_send, pos_recv.at[0], peer)
    for peer in line_peers:
        send(own_pos, lpos.at[line_slot], pos_send, pos_recv.at[1], peer)
    gather_start(0, b_ref, 0)
    gather_start(0, b_ref, 1)
    ppos[slot] = own_pos[...]
    lpos[line_slot] = own_pos[...]
    gath[0, slot] = b_ref[...]
    inverse_radii = 1.0 / own_pos[...].T[:, 3:4]

    wait(ppos.at[0 : PLANE - 1], pos_recv.at[0])
    wait(lpos.at[0 : LINE - 1], pos_recv.at[1])
    gather_forward(0)

    def spread(t, _):
        rows = pl.ds(pl.multiple_of(t * B, B), B)
        turned = lpos[t].T
        for c in range(3):
            xb[c, rows, :] = jnp.broadcast_to(turned[:, c : c + 1], (B, B))
        return 0

    lax.fori_loop(0, LINE, spread, 0)

    def evaluate(t, _):
        rows = pl.ds(pl.multiple_of(t * B, B), B)
        for j in range(PLANE):
            d0 = xb[0, rows, :] - ppos[j, 0:1, :]
            d1 = xb[1, rows, :] - ppos[j, 1:2, :]
            d2 = xb[2, rows, :] - ppos[j, 2:3, :]
            weight = lax.rsqrt(d0 * d0 + d1 * d1 + d2 * d2 + softening)
            high = weight.astype(BF16)
            khi[rows, j * B : (j + 1) * B] = high
            klo[rows, j * B : (j + 1) * B] = (weight - high.astype(F32)).astype(BF16)
        return 0

    lax.fori_loop(0, LINE, evaluate, 0)

    def split_values(m):
        def step(s, _):
            rows = pl.ds(pl.multiple_of(s * B, B), B)
            value = gath[m, s]
            high = value.astype(BF16)
            vhi[rows, :] = high
            vlo[rows, :] = (value - high.astype(F32)).astype(BF16)
            return 0

        lax.fori_loop(0, PLANE, step, 0)

    def sub_rows(c):
        return pl.ds(c * SR, SR)

    def ring_target(way, s):
        return at_z(4 - s) if way == 0 else at_z(4 + s)

    def ring_peer(way):
        return device(x, y, at_z(1 if way == 0 else NZ - 1), k)

    def join_sibling(m, dest):
        wait(sib.at[m, dest], s_recv.at[m, dest])
        mine = pl.ds(pl.multiple_of(dest * 2 * B + k * B, B), B)
        sib[m, dest] = sib[m, dest] + part[mine, :]

    def ring_step(m, s):
        if s == 0:
            for c in range(SUB // 2):
                for way in range(2):
                    cc = c if way == 0 else c + SUB // 2
                    piece = sib.at[m, ring_target(way, 0), sub_rows(cc)]
                    send(piece, ring.at[m, way, 0, sub_rows(cc)], r_send.at[m], r_recv.at[m, way, 0, cc], ring_peer(way))
            return
        late = ((0, 1), (2, 3))
        for i in range(SUB):
            for way in range(2):
                order = late[1 - way] + late[way]
                c = order[i]
                dest = ring_target(way, s)
                if s == 1 and c not in late[way]:
                    piece = sib.at[m, dest, sub_rows(c)]
                else:
                    piece = ring.at[m, way, s - 1, sub_rows(c)]
                    wait(piece, r_recv.at[m, way, s - 1, c])
                    piece[...] = piece[...] + sib[m, dest, sub_rows(c), :]
                send(piece, ring.at[m, way, s, sub_rows(c)], r_send.at[m], r_recv.at[m, way, s, c], ring_peer(way))

    def ring_result(m, c):
        for way in range(2):
            wait(ring.at[m, way, 3, sub_rows(c)], r_recv.at[m, way, 3, c])
        return sib[m, z, sub_rows(c), :] + ring[m, 0, 3, sub_rows(c), :] + ring[m, 1, 3, sub_rows(c), :]

    def products(m):
        def step(i, _):
            off = 4 + (1 - 2 * lax.rem(i, 2)) * ((i + 1) // 2)
            dest = at_z(off)
            rows = pl.ds(pl.multiple_of(dest * 2 * B, 2 * B), 2 * B)
            high = khi[rows, :]
            total = jnp.dot(klo[rows, :], vhi[...], preferred_element_type=F32)
            total = total + jnp.dot(high, vlo[...], preferred_element_type=F32)
            part[rows, :] = total + jnp.dot(high, vhi[...], preferred_element_type=F32)
            other = pl.ds(pl.multiple_of(dest * 2 * B + (1 - k) * B, B), B)
            send(part.at[other], sib.at[m, dest], s_send.at[m], s_recv.at[m, dest], sibling)

            @pl.when(i == 2)
            def _():
                join_sibling(m, at_z(4))
                ring_step(m, 0)

            return 0

        lax.fori_loop(0, NZ, step, 0)
        for d in (3, 5):
            join_sibling(m, at_z(d))
        ring_step(m, 1)
        for d in (2, 6, 1, 7, 0):
            join_sibling(m, at_z(d))

    gather_finish(0)
    split_values(0)
    products(0)
    ring_step(0, 2)
    ring_step(0, 3)
    for h in range(2):
        for c in range(h * SUB // 2, (h + 1) * SUB // 2):
            rows = slice(c * SR, (c + 1) * SR)
            w1[rows, :] = b_ref[rows, :] * inverse_radii[rows] + kernel_scale * ring_result(0, c)
        gather_start(1, w1, h)
    gath[1, slot] = w1[...]
    b = b_ref[...]
    ar_src[0] = jnp.zeros((8, R), F32)
    ar_src[0, 0:1, :] = jnp.sum(b * b, axis=0, keepdims=True)
    ar_src[0, 1:2, :] = jnp.sum(b * w1[...], axis=0, keepdims=True)
    sum_start(0)
    wait(gath.at[0, 0:NZ], s_send.at[0])
    gather_forward(1)
    sum_middle(0)
    gather_finish(1)
    split_values(1)
    sums = sum_finish(0)
    norm0 = sums[0:1, :]
    alpha = norm0 / sums[1:2, :]
    r1[...] = b_ref[...] - alpha * w1[...]
    ar_src[1] = jnp.zeros((8, R), F32)
    ar_src[1, 0:1, :] = jnp.sum(r1[...] * r1[...], axis=0, keepdims=True)
    sum_start(1)
    products(1)
    sum_middle(1)
    ring_step(1, 2)
    ring_step(1, 3)
    norm1 = sum_finish(1)[0:1, :]
    beta = norm1 / norm0
    for c in range(SUB):
        rows = slice(c * SR, (c + 1) * SR)
        w2[rows, :] = w1[rows, :] * inverse_radii[rows] + kernel_scale * ring_result(1, c)
    direction = r1[...] + beta * b_ref[...]
    w2[...] = (1.0 + beta) * w1[...] - alpha * w2[...]
    ar_src[2] = jnp.zeros((8, R), F32)
    ar_src[2, 0:1, :] = jnp.sum(direction * w2[...], axis=0, keepdims=True)
    sum_start(2)
    sum_middle(2)
    step_size = norm1 / sum_finish(2)[0:1, :]
    sol_ref[...] = alpha * b_ref[...] + step_size * (r1[...] + beta * b_ref[...])
    res_ref[...] = r1[...] - step_size * w2[...]

    wait(ar_plane.at[0, 0 : PLANE - 1], pos_send)
    for m in range(2):
        wait(gath.at[m, 0 : PLANE - 1], g_send.at[m])
        wait(gath.at[m, 0 : NZ - 1], r_send.at[m])
    wait(gath.at[1, 0:NZ], s_send.at[1])
    for i in range(3):
        wait(ar_line.at[i, 0 : LINE - 1], ar_send.at[i, 1])


def body(positions, radii, right_side):
    total = B * lax.axis_size("row") * lax.axis_size("col")
    kernel_scale, softening = constants(total)
    vmem = pl.BlockSpec(memory_space=pltpu.VMEM)
    out = jax.ShapeDtypeStruct((B, R), F32)
    dma = pltpu.SemaphoreType.DMA
    cols = PLANE * B
    return pl.pallas_call(
        functools.partial(kernel, kernel_scale, softening),
        out_shape=(out, out),
        in_specs=[vmem] * 3,
        out_specs=(vmem, vmem),
        scratch_shapes=[
            pltpu.VMEM((LINE * B, cols), BF16),
            pltpu.VMEM((LINE * B, cols), BF16),
            pltpu.VMEM((2, PLANE, B, R), F32),
            pltpu.VMEM((cols, R), BF16),
            pltpu.VMEM((cols, R), BF16),
            pltpu.VMEM((LINE * B, R), F32),
            pltpu.VMEM((2, NZ, B, R), F32),
            pltpu.VMEM((2, 2, 4, B, R), F32),
            pltpu.VMEM((3, LINE * B, B), F32),
            pltpu.VMEM((PLANE, 8, B), F32),
            pltpu.VMEM((LINE, 8, B), F32),
            pltpu.VMEM((8, B), F32),
            pltpu.VMEM((B, R), F32),
            pltpu.VMEM((B, R), F32),
            pltpu.VMEM((B, R), F32),
            pltpu.VMEM((3, 8, R), F32),
            pltpu.VMEM((3, PLANE, 8, R), F32),
            pltpu.VMEM((3, LINE, 8, R), F32),
            dma,
            dma((2,)),
            dma((2,)),
            dma((2, 2, PLANE)),
            dma((2,)),
            dma((2, NZ)),
            dma((2,)),
            dma((2, 2, 4, SUB)),
            dma((3, 2)),
            dma((3, 2)),
        ],
        compiler_params=pltpu.CompilerParams(
            collective_id=0, has_side_effects=True, vmem_limit_bytes=56 << 20
        ),
        name="cg",
    )(positions, radii.reshape(1, B), right_side)


def solution(mesh):
    return jax.shard_map(
        body,
        mesh=mesh,
        in_specs=(P(None, ("row", "col")), P(("row", "col")), P(("row", "col"), None)),
        out_specs=(P(("row", "col"), None), P(("row", "col"), None)),
        check_vma=False,
    )
```

```python
import functools

import jax
import jax.numpy as jnp
from jax import lax
from jax.experimental import pallas as pl
from jax.experimental.pallas import tpu as pltpu
from jax.sharding import PartitionSpec as P

MESH = pl.DeviceIdType.MESH
B = 128
R = 256
NX, NY, NZ = 4, 4, 8
PLANE = NX * NY
LINE = NZ * 2
HALF = B // 2
SUB = 4
SR = B // SUB
F32 = jnp.float32
BF16 = jnp.bfloat16


def constants(total):
    kernel_scale = float(total) ** (-0.5)
    spacing = 0.25 * float(total) ** (-1.0 / 3.0)
    return (kernel_scale, spacing * spacing)


def kernel(
    kernel_scale, softening,
    pos_ref, rad_ref, b_ref, sol_ref, res_ref,
    khi, klo, gath, vhi, vlo, part, sib, ring, xb, ppos, lpos, own_pos, inv, w1, ar_src, ar_plane, ar_line,
    pos_send, pos_recv, g_send, g_recv, q_recv, s_send, s_recv, r_send, r_recv, ar_send, ar_recv,
):
    row, col = lax.axis_index("row"), lax.axis_index("col")
    x, y = col // 4, lax.rem(row, 4)
    z, k = (row // 4) * 2 + lax.rem(col // 2, 2), lax.rem(col, 2)

    def device(xx, yy, zz, kk):
        return {"row": (zz // 2) * 4 + yy, "col": xx * 4 + lax.rem(zz, 2) * 2 + kk}

    def at_x(d):
        return lax.rem(x + d, NX)

    def at_y(d):
        return lax.rem(y + d, NY)

    def at_z(d):
        return lax.rem(z + d, NZ)

    def send(src, dst, ssem, rsem, dev):
        pltpu.make_async_remote_copy(
            src_ref=src, dst_ref=dst, send_sem=ssem, recv_sem=rsem, device_id=dev, device_id_type=MESH
        ).start()

    def wait(ref, sem):
        pltpu.make_async_copy(ref, ref, sem).wait()

    plane_peers = [device(at_x(dx), at_y(dy), z, k) for dx in range(NX) for dy in range(NY) if dx or dy]
    line_peers = [
        device(x, y, at_z(dz), lax.rem(k + dk, 2)) for dz in range(NZ) for dk in range(2) if dz or dk
    ]
    sibling = device(x, y, z, 1 - k)
    slot = x * NY + y
    line_slot = z * 2 + k

    barrier = pltpu.get_barrier_semaphore()
    for peer in plane_peers + line_peers:
        pl.semaphore_signal(barrier, 1, device_id=peer, device_id_type=MESH)
    own_pos[...] = jnp.zeros_like(own_pos)
    own_pos[0:3, :] = pos_ref[...]
    own_pos[3:4, :] = rad_ref[...]
    pl.semaphore_wait(barrier, len(plane_peers) + len(line_peers))

    def half_rows(h):
        return pl.ds(h * HALF, HALF)

    def plane_slot(h, first, second):
        return at_x(first) * NY + at_y(second) if h == 0 else at_x(second) * NY + at_y(first)

    def first_peer(h, d):
        return device(at_x(d), y, z, k) if h == 0 else device(x, at_y(d), z, k)

    def second_peer(h, d):
        return device(x, at_y(d), z, k) if h == 0 else device(at_x(d), y, z, k)

    def first_at(h, d):
        return at_x(d) if h == 0 else at_y(d)

    def gather_start(m, src, h):
        for d in (2, 1, 3):
            send(src.at[half_rows(h)], gath.at[m, slot, half_rows(h)], g_send.at[m], g_recv.at[m, h, slot], first_peer(h, d))
        for d in (1, 3):
            send(src.at[half_rows(h)], gath.at[m, slot, half_rows(h)], g_send.at[m], g_recv.at[m, h, slot], second_peer(h, d))

    def gather_spread(m):
        for o in (1, 3, 2):
            for h in range(2):
                s = plane_slot(h, o, 0)
                piece = gath.at[m, s, half_rows(h)]
                wait(piece, g_recv.at[m, h, s])
                for d in (1, 3):
                    send(piece, piece, g_send.at[m], g_recv.at[m, h, s], second_peer(h, d))

    def quarter(m, h, s, q):
        return gath.at[m, s, pl.ds(h * HALF + q * HALF // 2, HALF // 2)]

    def gather_forward(m, offsets):
        for o in offsets:
            for h in range(2):
                for q in range(2):
                    s = plane_slot(h, o, 3 if q == 0 else 1)
                    wait(gath.at[m, s, half_rows(h)], g_recv.at[m, h, s])
                    piece = quarter(m, h, s, q)
                    send(piece, piece, g_send.at[m], q_recv.at[m, h, q, first_at(h, o)], second_peer(h, 1 if q == 0 else 3))

    def gather_finish(m):
        for o in (0, 1, 3, 2):
            for h in range(2):
                for q in range(2):
                    wait(quarter(m, h, plane_slot(h, o, 2), q), q_recv.at[m, h, q, first_at(h, o)])

    def pack(i, j, term):
        column = jnp.sum(term, axis=0, keepdims=True)
        ar_src[i, 2 * j : 2 * j + 1, :] = column[:, :B]
        ar_src[i, 2 * j + 1 : 2 * j + 2, :] = column[:, B:]

    def unpack(total, j):
        return jnp.concatenate([total[2 * j : 2 * j + 1, :], total[2 * j + 1 : 2 * j + 2, :]], axis=1)

    def sum_start(i):
        ar_plane[i, slot] = ar_src[i]
        for peer in plane_peers:
            send(ar_src.at[i], ar_plane.at[i, slot], ar_send.at[i, 0], ar_recv.at[i, 0], peer)

    def sum_middle(i):
        wait(ar_plane.at[i, 0 : PLANE - 1], ar_send.at[i, 0])
        wait(ar_plane.at[i, 0 : PLANE - 1], ar_recv.at[i, 0])
        total = ar_plane[i, 0]
        for s in range(1, PLANE):
            total = total + ar_plane[i, s]
        ar_src[i] = total
        ar_line[i, line_slot] = total
        for peer in line_peers:
            send(ar_src.at[i], ar_line.at[i, line_slot], ar_send.at[i, 1], ar_recv.at[i, 1], peer)

    def sum_finish(i):
        wait(ar_line.at[i, 0 : LINE - 1], ar_recv.at[i, 1])
        total = ar_line[i, 0]
        for s in range(1, LINE):
            total = total + ar_line[i, s]
        return total

    for peer in line_peers:
        send(own_pos, lpos.at[line_slot], pos_send, pos_recv.at[1], peer)
    for peer in plane_peers:
        send(own_pos, ppos.at[slot], pos_send, pos_recv.at[0], peer)
    gather_start(0, b_ref, 0)
    gather_start(0, b_ref, 1)
    ppos[slot] = own_pos[...]
    lpos[line_slot] = own_pos[...]
    gath[0, slot] = b_ref[...]
    inv[...] = jnp.broadcast_to(1.0 / own_pos[3:4, :], (B, B)).T
    gather_spread(0)
    wait(lpos.at[0 : LINE - 1], pos_recv.at[1])

    def spread(t, _):
        for u in range(4):
            rows = pl.ds(pl.multiple_of(t * 4 * B + u * B, B), B)
            for a in range(3):
                xb[a, rows, :] = jnp.broadcast_to(lpos[t * 4 + u, a : a + 1, :], (B, B)).T
        return 0

    lax.fori_loop(0, LINE // 4, spread, 0)
    gather_forward(0, (0,))
    wait(ppos.at[0 : PLANE - 1], pos_recv.at[0])

    def evaluate(t, _):
        rows = pl.ds(pl.multiple_of(t * B, B), B)
        for j in range(PLANE):
            d0 = xb[0, rows, :] - ppos[j, 0:1, :]
            d1 = xb[1, rows, :] - ppos[j, 1:2, :]
            d2 = xb[2, rows, :] - ppos[j, 2:3, :]
            weight = lax.rsqrt(d0 * d0 + d1 * d1 + d2 * d2 + softening)
            high = weight.astype(BF16)
            khi[rows, j * B : (j + 1) * B] = high
            klo[rows, j * B : (j + 1) * B] = (weight - high.astype(F32)).astype(BF16)
        return 0

    lax.fori_loop(0, 6, evaluate, 0)
    gather_forward(0, (1, 3))
    lax.fori_loop(6, 12, evaluate, 0)
    gather_forward(0, (2,))
    lax.fori_loop(12, LINE, evaluate, 0)

    def split_values(m):
        def step(s, _):
            rows = pl.ds(pl.multiple_of(s * B, B), B)
            value = gath[m, s]
            high = value.astype(BF16)
            vhi[rows, :] = high
            vlo[rows, :] = (value - high.astype(F32)).astype(BF16)
            return 0

        lax.fori_loop(0, PLANE, step, 0)

    def sub_rows(c):
        return pl.ds(c * SR, SR)

    def ring_target(way, s):
        return at_z(4 - s) if way == 0 else at_z(4 + s)

    def ring_peer(way):
        return device(x, y, at_z(1 if way == 0 else NZ - 1), k)

    def join_sibling(m, dest):
        wait(sib.at[m, dest], s_recv.at[m, dest])
        mine = pl.ds(pl.multiple_of(dest * 2 * B + k * B, B), B)
        sib[m, dest] = sib[m, dest] + part[mine, :]

    def ring_step(m, s):
        if s == 0:
            for c in range(SUB // 2):
                for way in range(2):
                    cc = c if way == 0 else c + SUB // 2
                    piece = sib.at[m, ring_target(way, 0), sub_rows(cc)]
                    send(piece, ring.at[m, way, 0, sub_rows(cc)], r_send.at[m], r_recv.at[m, way, 0, cc], ring_peer(way))
            return
        late = ((0, 1), (2, 3))
        for i in range(SUB):
            for way in range(2):
                order = late[1 - way] + late[way]
                c = order[i]
                dest = ring_target(way, s)
                if s == 1 and c not in late[way]:
                    piece = sib.at[m, dest, sub_rows(c)]
                else:
                    piece = ring.at[m, way, s - 1, sub_rows(c)]
                    wait(piece, r_recv.at[m, way, s - 1, c])
                    piece[...] = piece[...] + sib[m, dest, sub_rows(c), :]
                send(piece, ring.at[m, way, s, sub_rows(c)], r_send.at[m], r_recv.at[m, way, s, c], ring_peer(way))

    def ring_result(m, c):
        for way in range(2):
            wait(ring.at[m, way, 3, sub_rows(c)], r_recv.at[m, way, 3, c])
        return sib[m, z, sub_rows(c), :] + ring[m, 0, 3, sub_rows(c), :] + ring[m, 1, 3, sub_rows(c), :]

    def products(m):
        def step(i, _):
            off = 4 + (1 - 2 * lax.rem(i, 2)) * ((i + 1) // 2)
            dest = at_z(off)
            rows = pl.ds(pl.multiple_of(dest * 2 * B, 2 * B), 2 * B)
            high = khi[rows, :]
            total = jnp.dot(klo[rows, :], vhi[...], preferred_element_type=F32)
            total = total + jnp.dot(high, vlo[...], preferred_element_type=F32)
            part[rows, :] = total + jnp.dot(high, vhi[...], preferred_element_type=F32)
            other = pl.ds(pl.multiple_of(dest * 2 * B + (1 - k) * B, B), B)
            send(part.at[other], sib.at[m, dest], s_send.at[m], s_recv.at[m, dest], sibling)

            for at, work in hooks:
                pl.when(i == at)(work)

            return 0

        def first():
            join_sibling(m, at_z(4))
            ring_step(m, 0)

        def second():
            join_sibling(m, at_z(3))
            join_sibling(m, at_z(5))
            ring_step(m, 1)

        hooks = ((1, first), (4, second))
        lax.fori_loop(0, NZ, step, 0)
        for d in (2, 6):
            join_sibling(m, at_z(d))
        ring_step(m, 2)
        for d in (1, 7):
            join_sibling(m, at_z(d))
        ring_step(m, 3)
        join_sibling(m, z)

    ar_src[...] = jnp.zeros_like(ar_src)
    gather_finish(0)
    split_values(0)
    products(0)
    pack(0, 0, b_ref[...] * b_ref[...])
    for h in range(2):
        for c in range(h * SUB // 2, (h + 1) * SUB // 2):
            rows = slice(c * SR, (c + 1) * SR)
            own = jnp.concatenate([inv[rows, :], inv[rows, :]], axis=1) * b_ref[rows, :]
            w1[rows, :] = own + kernel_scale * ring_result(0, c)
        gather_start(1, w1, h)
    gath[1, slot] = w1[...]
    pack(0, 1, b_ref[...] * w1[...])
    sum_start(0)
    wait(gath.at[0, 0:NZ], s_send.at[0])
    gather_spread(1)
    gather_forward(1, (0, 1, 3))
    sum_middle(0)
    gather_forward(1, (2,))
    gather_finish(1)
    split_values(1)
    products(1)
    sums = sum_finish(0)
    norm0 = unpack(sums, 0)
    curvature = unpack(sums, 1)
    alpha = norm0 / curvature
    r = b_ref[...] - alpha * w1[...]
    sol_ref[...] = r
    res_ref[...] = w1[...] - alpha * (
        jnp.concatenate([inv[...], inv[...]], axis=1) * w1[...] + kernel_scale * sib[1, z]
    )
    pack(1, 0, r * r)
    pack(1, 2, w1[...] * r)
    for c in range(SUB):
        for way in range(2):
            wait(ring.at[1, way, 3, sub_rows(c)], r_recv.at[1, way, 3, c])
    ar = res_ref[...] - (kernel_scale * alpha) * (ring[1, 0, 3] + ring[1, 1, 3])
    res_ref[...] = ar
    pack(1, 1, sol_ref[...] * ar)
    sum_start(1)
    sum_middle(1)
    sums = sum_finish(1)
    norm1 = unpack(sums, 0)
    beta = norm1 / norm0
    step_size = norm1 / (unpack(sums, 1) + 2.0 * beta * unpack(sums, 2) + beta * beta * curvature)
    r = sol_ref[...]
    sol_ref[...] = alpha * b_ref[...] + step_size * (r + beta * b_ref[...])
    res_ref[...] = r - step_size * (res_ref[...] + beta * w1[...])

    wait(gath.at[0, 0, 0 : B - 8], pos_send)
    for m in range(2):
        wait(gath.at[m, 0 : PLANE - 1], g_send.at[m])
        wait(gath.at[m, 0 : NZ - 1], r_send.at[m])
    wait(gath.at[1, 0:NZ], s_send.at[1])
    for i in range(2):
        wait(ar_line.at[i, 0 : LINE - 1], ar_send.at[i, 1])


def body(positions, radii, right_side):
    total = B * lax.axis_size("row") * lax.axis_size("col")
    kernel_scale, softening = constants(total)
    vmem = pl.BlockSpec(memory_space=pltpu.VMEM)
    out = jax.ShapeDtypeStruct((B, R), F32)
    dma = pltpu.SemaphoreType.DMA
    cols = PLANE * B
    return pl.pallas_call(
        functools.partial(kernel, kernel_scale, softening),
        out_shape=(out, out),
        in_specs=[vmem] * 3,
        out_specs=(vmem, vmem),
        scratch_shapes=[
            pltpu.VMEM((LINE * B, cols), BF16),
            pltpu.VMEM((LINE * B, cols), BF16),
            pltpu.VMEM((2, PLANE, B, R), F32),
            pltpu.VMEM((cols, R), BF16),
            pltpu.VMEM((cols, R), BF16),
            pltpu.VMEM((LINE * B, R), F32),
            pltpu.VMEM((2, NZ, B, R), F32),
            pltpu.VMEM((2, 2, 4, B, R), F32),
            pltpu.VMEM((3, LINE * B, B), F32),
            pltpu.VMEM((PLANE, 8, B), F32),
            pltpu.VMEM((LINE, 8, B), F32),
            pltpu.VMEM((8, B), F32),
            pltpu.VMEM((B, B), F32),
            pltpu.VMEM((B, R), F32),
            pltpu.VMEM((2, 8, B), F32),
            pltpu.VMEM((2, PLANE, 8, B), F32),
            pltpu.VMEM((2, LINE, 8, B), F32),
            dma,
            dma((2,)),
            dma((2,)),
            dma((2, 2, PLANE)),
            dma((2, 2, 2, NX)),
            dma((2,)),
            dma((2, NZ)),
            dma((2,)),
            dma((2, 2, 4, SUB)),
            dma((2, 2)),
            dma((2, 2)),
        ],
        compiler_params=pltpu.CompilerParams(
            collective_id=0, has_side_effects=True, vmem_limit_bytes=56 << 20
        ),
        name="cg",
    )(positions, radii.reshape(1, B), right_side)


def solution(mesh):
    return jax.shard_map(
        body,
        mesh=mesh,
        in_specs=(P(None, ("row", "col")), P(("row", "col")), P(("row", "col"), None)),
        out_specs=(P(("row", "col"), None), P(("row", "col"), None)),
        check_vma=False,
    )
```

```python
import functools

import jax
import jax.numpy as jnp
from jax import lax
from jax.experimental import pallas as pl
from jax.experimental.pallas import tpu as pltpu
from jax.sharding import PartitionSpec as P

MESH = pl.DeviceIdType.MESH
B = 128
R = 256
NX, NY, NZ = 4, 4, 8
PLANE = NX * NY
LINE = NZ * 2
HALF = B // 2
SUB = 4
SR = B // SUB
F32 = jnp.float32
BF16 = jnp.bfloat16


def constants(total):
    kernel_scale = float(total) ** (-0.5)
    spacing = 0.25 * float(total) ** (-1.0 / 3.0)
    return (kernel_scale, spacing * spacing)


def kernel(
    kernel_scale, softening,
    pos_ref, rad_ref, b_ref, sol_ref, res_ref,
    khi, klo, gath, vhi, vlo, part, sib, ring, xb, ppos, lpos, own_pos, inv, w1, line, ar_src, ar_plane, ar_line,
    pos_send, pos_recv, g_send, g_recv, q_recv, l_send, l_recv, s_send, s_recv, r_send, r_recv, ar_send, ar_recv,
):
    row, col = lax.axis_index("row"), lax.axis_index("col")
    x, y = col // 4, lax.rem(row, 4)
    z, k = (row // 4) * 2 + lax.rem(col // 2, 2), lax.rem(col, 2)

    def device(xx, yy, zz, kk):
        return {"row": (zz // 2) * 4 + yy, "col": xx * 4 + lax.rem(zz, 2) * 2 + kk}

    def at_x(d):
        return lax.rem(x + d, NX)

    def at_y(d):
        return lax.rem(y + d, NY)

    def at_z(d):
        return lax.rem(z + d, NZ)

    def send(src, dst, ssem, rsem, dev):
        pltpu.make_async_remote_copy(
            src_ref=src, dst_ref=dst, send_sem=ssem, recv_sem=rsem, device_id=dev, device_id_type=MESH
        ).start()

    def wait(ref, sem):
        pltpu.make_async_copy(ref, ref, sem).wait()

    plane_peers = [device(at_x(dx), at_y(dy), z, k) for dx in range(NX) for dy in range(NY) if dx or dy]
    line_peers = [
        device(x, y, at_z(dz), lax.rem(k + dk, 2)) for dz in range(NZ) for dk in range(2) if dz or dk
    ]
    sibling = device(x, y, z, 1 - k)
    slot = x * NY + y
    line_slot = z * 2 + k

    barrier = pltpu.get_barrier_semaphore()
    for peer in plane_peers + line_peers:
        pl.semaphore_signal(barrier, 1, device_id=peer, device_id_type=MESH)
    own_pos[...] = jnp.zeros_like(own_pos)
    own_pos[0:3, :] = pos_ref[...]
    own_pos[3:4, :] = rad_ref[...]
    pl.semaphore_wait(barrier, len(plane_peers) + len(line_peers))

    def half_rows(h):
        return pl.ds(h * HALF, HALF)

    def plane_slot(h, first, second):
        return at_x(first) * NY + at_y(second) if h == 0 else at_x(second) * NY + at_y(first)

    def first_peer(h, d):
        return device(at_x(d), y, z, k) if h == 0 else device(x, at_y(d), z, k)

    def second_peer(h, d):
        return device(x, at_y(d), z, k) if h == 0 else device(at_x(d), y, z, k)

    def first_at(h, d):
        return at_x(d) if h == 0 else at_y(d)

    def gather_start(m, src, h):
        for d in (1, 3, 2):
            send(src.at[half_rows(h)], gath.at[m, slot, half_rows(h)], g_send.at[m], g_recv.at[m, h, slot], first_peer(h, d))

    def gather_second(m, src, h):
        for d in (1, 3):
            send(src.at[half_rows(h)], gath.at[m, slot, half_rows(h)], g_send.at[m], g_recv.at[m, h, slot], second_peer(h, d))

    def gather_spread(m):
        for o in (1, 3, 2):
            for h in range(2):
                s = plane_slot(h, o, 0)
                piece = gath.at[m, s, half_rows(h)]
                wait(piece, g_recv.at[m, h, s])
                for d in (1, 3):
                    send(piece, piece, g_send.at[m], g_recv.at[m, h, s], second_peer(h, d))

    def quarter(m, h, s, q):
        return gath.at[m, s, pl.ds(h * HALF + q * HALF // 2, HALF // 2)]

    def gather_forward(m, offsets):
        for o in offsets:
            for h in range(2):
                for q in range(2):
                    s = plane_slot(h, o, 3 if q == 0 else 1)
                    wait(gath.at[m, s, half_rows(h)], g_recv.at[m, h, s])
                    piece = quarter(m, h, s, q)
                    send(piece, piece, g_send.at[m], q_recv.at[m, h, q, first_at(h, o)], second_peer(h, 1 if q == 0 else 3))

    def gather_finish(m):
        for o in (0, 1, 3, 2):
            for h in range(2):
                for q in range(2):
                    wait(quarter(m, h, plane_slot(h, o, 2), q), q_recv.at[m, h, q, first_at(h, o)])

    def line_step(m, j):
        for p in range(2):
            for way in range(2):
                if j == 4 and p != way:
                    continue
                source = at_z(1 - j + NZ if way == 0 else j - 1)
                piece = line.at[m, source, half_rows(p)]
                if j > 1:
                    wait(piece, l_recv.at[m, source, p])
                peer = device(x, y, at_z(1 if way == 0 else NZ - 1), k)
                send(piece, piece, l_send.at[m], l_recv.at[m, source, p], peer)

    def line_finish(m):
        wait(line.at[m, at_z(5), half_rows(1)], l_recv.at[m, at_z(5), 1])
        wait(line.at[m, at_z(3), half_rows(0)], l_recv.at[m, at_z(3), 0])
        for p in range(2):
            wait(line.at[m, at_z(4), half_rows(p)], l_recv.at[m, at_z(4), p])

    def pack(i, j, term):
        column = jnp.sum(term, axis=0, keepdims=True)
        ar_src[i, 2 * j : 2 * j + 1, :] = column[:, :B]
        ar_src[i, 2 * j + 1 : 2 * j + 2, :] = column[:, B:]

    def unpack(total, j):
        return jnp.concatenate([total[2 * j : 2 * j + 1, :], total[2 * j + 1 : 2 * j + 2, :]], axis=1)

    def sum_start(i):
        ar_plane[i, slot] = ar_src[i]
        for peer in plane_peers:
            send(ar_src.at[i], ar_plane.at[i, slot], ar_send.at[i, 0], ar_recv.at[i, 0], peer)

    def sum_middle(i):
        wait(ar_plane.at[i, 0 : PLANE - 1], ar_send.at[i, 0])
        wait(ar_plane.at[i, 0 : PLANE - 1], ar_recv.at[i, 0])
        total = ar_plane[i, 0]
        for s in range(1, PLANE):
            total = total + ar_plane[i, s]
        ar_src[i] = total
        ar_line[i, line_slot] = total
        for peer in line_peers:
            send(ar_src.at[i], ar_line.at[i, line_slot], ar_send.at[i, 1], ar_recv.at[i, 1], peer)

    def sum_finish(i):
        wait(ar_line.at[i, 0 : LINE - 1], ar_recv.at[i, 1])
        total = ar_line[i, 0]
        for s in range(1, LINE):
            total = total + ar_line[i, s]
        return total

    for peer in line_peers:
        send(own_pos, lpos.at[line_slot], pos_send, pos_recv.at[1], peer)
    for peer in plane_peers:
        send(own_pos, ppos.at[slot], pos_send, pos_recv.at[0], peer)
    for h in range(2):
        gather_start(0, b_ref, h)
    for h in range(2):
        gather_second(0, b_ref, h)
    line[0, z] = b_ref[...]
    line_step(0, 1)
    ppos[slot] = own_pos[...]
    lpos[line_slot] = own_pos[...]
    gath[0, slot] = b_ref[...]
    inv[...] = jnp.broadcast_to(1.0 / own_pos[3:4, :], (B, B)).T
    gather_spread(0)
    wait(lpos.at[0 : LINE - 1], pos_recv.at[1])

    def spread(t, _):
        for u in range(4):
            rows = pl.ds(pl.multiple_of(t * 4 * B + u * B, B), B)
            for a in range(3):
                xb[a, rows, :] = jnp.broadcast_to(lpos[t * 4 + u, a : a + 1, :], (B, B)).T
        return 0

    lax.fori_loop(0, LINE // 4, spread, 0)
    gather_forward(0, (0,))
    wait(ppos.at[0 : PLANE - 1], pos_recv.at[0])

    def evaluate(t, _):
        rows = pl.ds(pl.multiple_of(t * B, B), B)
        for j in range(PLANE):
            d0 = xb[0, rows, :] - ppos[j, 0:1, :]
            d1 = xb[1, rows, :] - ppos[j, 1:2, :]
            d2 = xb[2, rows, :] - ppos[j, 2:3, :]
            weight = lax.rsqrt(d0 * d0 + d1 * d1 + d2 * d2 + softening)
            high = weight.astype(BF16)
            khi[rows, j * B : (j + 1) * B] = high
            klo[rows, j * B : (j + 1) * B] = (weight - high.astype(F32)).astype(BF16)
        return 0

    lax.fori_loop(0, 6, evaluate, 0)
    gather_forward(0, (1, 3))
    line_step(0, 2)
    lax.fori_loop(6, 12, evaluate, 0)
    gather_forward(0, (2,))
    line_step(0, 3)
    lax.fori_loop(12, LINE, evaluate, 0)

    def split_values(m):
        def step(s, _):
            rows = pl.ds(pl.multiple_of(s * B, B), B)
            value = gath[m, s]
            high = value.astype(BF16)
            vhi[rows, :] = high
            vlo[rows, :] = (value - high.astype(F32)).astype(BF16)
            return 0

        lax.fori_loop(0, PLANE, step, 0)

    def sub_rows(c):
        return pl.ds(c * SR, SR)

    def ring_target(way, s):
        return at_z(4 - s) if way == 0 else at_z(4 + s)

    def ring_peer(way):
        return device(x, y, at_z(1 if way == 0 else NZ - 1), k)

    def join_sibling(m, dest):
        wait(sib.at[m, dest], s_recv.at[m, dest])
        mine = pl.ds(pl.multiple_of(dest * 2 * B + k * B, B), B)
        sib[m, dest] = sib[m, dest] + part[mine, :]

    def ring_step(m, s):
        for i in range(SUB):
            for way in range(2):
                c = 2 * (i % (SUB // 2)) + (1 - way if i < SUB // 2 else way)
                if s == 0 and c % 2 != way:
                    continue
                dest = ring_target(way, s)
                if s == 0 or (s == 1 and c % 2 != way):
                    piece = sib.at[m, dest, sub_rows(c)]
                else:
                    piece = ring.at[m, way, s - 1, sub_rows(c)]
                    wait(piece, r_recv.at[m, way, s - 1, c])
                    piece[...] = piece[...] + sib[m, dest, sub_rows(c), :]
                send(piece, ring.at[m, way, s, sub_rows(c)], r_send.at[m], r_recv.at[m, way, s, c], ring_peer(way))

    def ring_result(m, c):
        for way in range(2):
            wait(ring.at[m, way, 3, sub_rows(c)], r_recv.at[m, way, 3, c])
        return sib[m, z, sub_rows(c), :] + ring[m, 0, 3, sub_rows(c), :] + ring[m, 1, 3, sub_rows(c), :]

    def products(m):
        def step(i, _):
            off = 4 + (1 - 2 * lax.rem(i, 2)) * ((i + 1) // 2)
            dest = at_z(off)
            rows = pl.ds(pl.multiple_of(dest * 2 * B, 2 * B), 2 * B)
            high = khi[rows, :]
            total = jnp.dot(klo[rows, :], vhi[...], preferred_element_type=F32)
            total = total + jnp.dot(high, vlo[...], preferred_element_type=F32)
            part[rows, :] = total + jnp.dot(high, vhi[...], preferred_element_type=F32)
            other = pl.ds(pl.multiple_of(dest * 2 * B + (1 - k) * B, B), B)
            send(part.at[other], sib.at[m, dest], s_send.at[m], s_recv.at[m, dest], sibling)

            for at, work in hooks:
                pl.when(i == at)(work)

            return 0

        def first():
            join_sibling(m, at_z(4))
            ring_step(m, 0)

        def second():
            join_sibling(m, at_z(3))
            join_sibling(m, at_z(5))
            ring_step(m, 1)

        hooks = ((1, first), (4 if m == 0 else 6, second))
        lax.fori_loop(0, NZ, step, 0)
        for d in (2, 6):
            join_sibling(m, at_z(d))
        if m == 0:
            ring_step(m, 2)
        for d in (1, 7, 0):
            join_sibling(m, at_z(d))

    ar_src[...] = jnp.zeros_like(ar_src)
    line_step(0, 4)
    gather_finish(0)
    split_values(0)
    products(0)
    ring_step(0, 3)
    pack(0, 0, b_ref[...] * b_ref[...])
    for h in range(2):
        for c in range(h * SUB // 2, (h + 1) * SUB // 2):
            rows = slice(c * SR, (c + 1) * SR)
            own = jnp.concatenate([inv[rows, :], inv[rows, :]], axis=1) * b_ref[rows, :]
            w1[rows, :] = own + kernel_scale * ring_result(0, c)
        gather_start(1, w1, h)
    for h in range(2):
        gather_second(1, w1, h)
    line[1, z] = w1[...]
    line_step(1, 1)
    gath[1, slot] = w1[...]
    pack(0, 1, b_ref[...] * w1[...])
    wait(gath.at[0, 0:NZ], s_send.at[0])
    gather_spread(1)
    line_step(1, 2)
    sum_start(0)
    gather_forward(1, (0, 1, 3))
    line_step(1, 3)
    gather_forward(1, (2,))
    gather_finish(1)
    sum_middle(0)
    line_step(1, 4)
    split_values(1)
    line_finish(0)
    products(1)
    sums = sum_finish(0)
    norm0 = unpack(sums, 0)
    curvature = unpack(sums, 1)
    alpha = norm0 / curvature
    line_finish(1)
    r = b_ref[...] - alpha * w1[...]
    sol_ref[...] = r
    scaled = jnp.concatenate([inv[...], inv[...]], axis=1) * w1[...]

    def meet(dest, total):
        return total + (line[0, dest] - alpha * line[1, dest]) * sib[1, dest]

    met = lax.fori_loop(0, NZ, meet, jnp.zeros((B, R), F32))
    pack(1, 0, r * r)
    pack(1, 1, r * (w1[...] - alpha * scaled) - (kernel_scale * alpha) * met)
    pack(1, 2, w1[...] * r)
    sum_start(1)
    ring_step(1, 2)
    sum_middle(1)
    ring_step(1, 3)
    res_ref[...] = w1[...] - alpha * (scaled + kernel_scale * sib[1, z])
    for c in range(SUB):
        for way in range(2):
            wait(ring.at[1, way, 3, sub_rows(c)], r_recv.at[1, way, 3, c])
    res_ref[...] = res_ref[...] - (kernel_scale * alpha) * (ring[1, 0, 3] + ring[1, 1, 3])
    sums = sum_finish(1)
    norm1 = unpack(sums, 0)
    beta = norm1 / norm0
    step_size = norm1 / (unpack(sums, 1) + 2.0 * beta * unpack(sums, 2) + beta * beta * curvature)
    r = sol_ref[...]
    sol_ref[...] = alpha * b_ref[...] + step_size * (r + beta * b_ref[...])
    res_ref[...] = r - step_size * (res_ref[...] + beta * w1[...])

    wait(gath.at[0, 0, 0 : B - 8], pos_send)
    for m in range(2):
        wait(gath.at[m, 0 : PLANE - 1], g_send.at[m])
        wait(gath.at[m, 0 : NZ - 1], r_send.at[m])
        wait(gath.at[m, 0 : NZ - 1], l_send.at[m])
    wait(gath.at[1, 0:NZ], s_send.at[1])
    for i in range(2):
        wait(ar_line.at[i, 0 : LINE - 1], ar_send.at[i, 1])


def body(positions, radii, right_side):
    total = B * lax.axis_size("row") * lax.axis_size("col")
    kernel_scale, softening = constants(total)
    vmem = pl.BlockSpec(memory_space=pltpu.VMEM)
    out = jax.ShapeDtypeStruct((B, R), F32)
    dma = pltpu.SemaphoreType.DMA
    cols = PLANE * B
    return pl.pallas_call(
        functools.partial(kernel, kernel_scale, softening),
        out_shape=(out, out),
        in_specs=[vmem] * 3,
        out_specs=(vmem, vmem),
        scratch_shapes=[
            pltpu.VMEM((LINE * B, cols), BF16),
            pltpu.VMEM((LINE * B, cols), BF16),
            pltpu.VMEM((2, PLANE, B, R), F32),
            pltpu.VMEM((cols, R), BF16),
            pltpu.VMEM((cols, R), BF16),
            pltpu.VMEM((LINE * B, R), F32),
            pltpu.VMEM((2, NZ, B, R), F32),
            pltpu.VMEM((2, 2, 4, B, R), F32),
            pltpu.VMEM((3, LINE * B, B), F32),
            pltpu.VMEM((PLANE, 8, B), F32),
            pltpu.VMEM((LINE, 8, B), F32),
            pltpu.VMEM((8, B), F32),
            pltpu.VMEM((B, B), F32),
            pltpu.VMEM((B, R), F32),
            pltpu.VMEM((2, NZ, B, R), F32),
            pltpu.VMEM((2, 8, B), F32),
            pltpu.VMEM((2, PLANE, 8, B), F32),
            pltpu.VMEM((2, LINE, 8, B), F32),
            dma,
            dma((2,)),
            dma((2,)),
            dma((2, 2, PLANE)),
            dma((2, 2, 2, NX)),
            dma((2,)),
            dma((2, NZ, 2)),
            dma((2,)),
            dma((2, NZ)),
            dma((2,)),
            dma((2, 2, 4, SUB)),
            dma((2, 2)),
            dma((2, 2)),
        ],
        compiler_params=pltpu.CompilerParams(
            collective_id=0, has_side_effects=True, vmem_limit_bytes=56 << 20
        ),
        name="cg",
    )(positions, radii.reshape(1, B), right_side)


def solution(mesh):
    return jax.shard_map(
        body,
        mesh=mesh,
        in_specs=(P(None, ("row", "col")), P(("row", "col")), P(("row", "col"), None)),
        out_specs=(P(("row", "col"), None), P(("row", "col"), None)),
        check_vma=False,
    )
```

```python
import functools

import jax
import jax.numpy as jnp
from jax import lax
from jax.experimental import pallas as pl
from jax.experimental.pallas import tpu as pltpu
from jax.sharding import PartitionSpec as P

MESH = pl.DeviceIdType.MESH
B = 128
R = 256
NX, NY, NZ = 4, 4, 8
PLANE = NX * NY
LINE = NZ * 2
HALF = B // 2
SUB = 4
SR = B // SUB
F32 = jnp.float32
BF16 = jnp.bfloat16


def constants(total):
    kernel_scale = float(total) ** (-0.5)
    spacing = 0.25 * float(total) ** (-1.0 / 3.0)
    return (kernel_scale, spacing * spacing)


def kernel(
    kernel_scale, softening,
    pos_ref, rad_ref, b_ref, sol_ref, res_ref,
    khi, klo, gath, vhi, vlo, part, sib, ring, xb, ppos, lpos, own_pos, inv, w1, line, ar_src, ar_plane, ar_line,
    pos_send, pos_recv, g_send, g_recv, q_recv, l_send, l_recv, s_send, s_recv, r_send, r_recv, ar_send, ar_recv,
):
    row, col = lax.axis_index("row"), lax.axis_index("col")
    x, y = col // 4, lax.rem(row, 4)
    z, k = (row // 4) * 2 + lax.rem(col // 2, 2), lax.rem(col, 2)

    def device(xx, yy, zz, kk):
        return {"row": (zz // 2) * 4 + yy, "col": xx * 4 + lax.rem(zz, 2) * 2 + kk}

    def at_x(d):
        return lax.rem(x + d, NX)

    def at_y(d):
        return lax.rem(y + d, NY)

    def at_z(d):
        return lax.rem(z + d, NZ)

    def send(src, dst, ssem, rsem, dev):
        pltpu.make_async_remote_copy(
            src_ref=src, dst_ref=dst, send_sem=ssem, recv_sem=rsem, device_id=dev, device_id_type=MESH
        ).start()

    def wait(ref, sem):
        pltpu.make_async_copy(ref, ref, sem).wait()

    plane_peers = [device(at_x(dx), at_y(dy), z, k) for dx in range(NX) for dy in range(NY) if dx or dy]
    line_peers = [
        device(x, y, at_z(dz), lax.rem(k + dk, 2)) for dz in range(NZ) for dk in range(2) if dz or dk
    ]
    sibling = device(x, y, z, 1 - k)
    slot = x * NY + y
    line_slot = z * 2 + k

    barrier = pltpu.get_barrier_semaphore()
    for peer in plane_peers + line_peers:
        pl.semaphore_signal(barrier, 1, device_id=peer, device_id_type=MESH)
    own_pos[...] = jnp.zeros_like(own_pos)
    own_pos[0:3, :] = pos_ref[...]
    own_pos[3:4, :] = rad_ref[...]
    pl.semaphore_wait(barrier, len(plane_peers) + len(line_peers))

    def half_rows(h):
        return pl.ds(h * HALF, HALF)

    def plane_slot(h, first, second):
        return at_x(first) * NY + at_y(second) if h == 0 else at_x(second) * NY + at_y(first)

    def first_peer(h, d):
        return device(at_x(d), y, z, k) if h == 0 else device(x, at_y(d), z, k)

    def second_peer(h, d):
        return device(x, at_y(d), z, k) if h == 0 else device(at_x(d), y, z, k)

    def first_at(h, d):
        return at_x(d) if h == 0 else at_y(d)

    def gather_start(m, src, h):
        for d in (1, 3, 2):
            send(src.at[half_rows(h)], gath.at[m, slot, half_rows(h)], g_send.at[m], g_recv.at[m, h, slot], first_peer(h, d))

    def gather_second(m, src, h):
        for d in (1, 3):
            send(src.at[half_rows(h)], gath.at[m, slot, half_rows(h)], g_send.at[m], g_recv.at[m, h, slot], second_peer(h, d))

    def gather_spread(m):
        for o in (1, 3, 2):
            for h in range(2):
                s = plane_slot(h, o, 0)
                piece = gath.at[m, s, half_rows(h)]
                wait(piece, g_recv.at[m, h, s])
                for d in (1, 3):
                    send(piece, piece, g_send.at[m], g_recv.at[m, h, s], second_peer(h, d))

    def quarter(m, h, s, q):
        return gath.at[m, s, pl.ds(h * HALF + q * HALF // 2, HALF // 2)]

    def gather_forward(m, offsets):
        for o in offsets:
            for h in range(2):
                for q in range(2):
                    s = plane_slot(h, o, 3 if q == 0 else 1)
                    wait(gath.at[m, s, half_rows(h)], g_recv.at[m, h, s])
                    piece = quarter(m, h, s, q)
                    send(piece, piece, g_send.at[m], q_recv.at[m, h, q, first_at(h, o)], second_peer(h, 1 if q == 0 else 3))

    def gather_finish(m):
        for o in (0, 1, 3, 2):
            for h in range(2):
                for q in range(2):
                    wait(quarter(m, h, plane_slot(h, o, 2), q), q_recv.at[m, h, q, first_at(h, o)])

    def line_step(m, j):
        for p in range(2):
            for way in range(2):
                if j == 4 and p != way:
                    continue
                source = at_z(1 - j + NZ if way == 0 else j - 1)
                piece = line.at[m, source, half_rows(p)]
                if j > 1:
                    wait(piece, l_recv.at[m, source, p])
                peer = device(x, y, at_z(1 if way == 0 else NZ - 1), k)
                send(piece, piece, l_send.at[m], l_recv.at[m, source, p], peer)

    def line_finish(m):
        wait(line.at[m, at_z(5), half_rows(1)], l_recv.at[m, at_z(5), 1])
        wait(line.at[m, at_z(3), half_rows(0)], l_recv.at[m, at_z(3), 0])
        for p in range(2):
            wait(line.at[m, at_z(4), half_rows(p)], l_recv.at[m, at_z(4), p])

    def pack(i, j, term):
        column = jnp.sum(term, axis=0, keepdims=True)
        ar_src[i, 2 * j : 2 * j + 1, :] = column[:, :B]
        ar_src[i, 2 * j + 1 : 2 * j + 2, :] = column[:, B:]

    def unpack(total, j):
        return jnp.concatenate([total[2 * j : 2 * j + 1, :], total[2 * j + 1 : 2 * j + 2, :]], axis=1)

    def sum_start(i):
        ar_plane[i, slot] = ar_src[i]
        for peer in plane_peers:
            send(ar_src.at[i], ar_plane.at[i, slot], ar_send.at[i, 0], ar_recv.at[i, 0], peer)

    def sum_middle(i):
        wait(ar_plane.at[i, 0 : PLANE - 1], ar_send.at[i, 0])
        wait(ar_plane.at[i, 0 : PLANE - 1], ar_recv.at[i, 0])
        total = ar_plane[i, 0]
        for s in range(1, PLANE):
            total = total + ar_plane[i, s]
        ar_src[i] = total
        ar_line[i, line_slot] = total
        for peer in line_peers:
            send(ar_src.at[i], ar_line.at[i, line_slot], ar_send.at[i, 1], ar_recv.at[i, 1], peer)

    def sum_finish(i):
        wait(ar_line.at[i, 0 : LINE - 1], ar_recv.at[i, 1])
        total = ar_line[i, 0]
        for s in range(1, LINE):
            total = total + ar_line[i, s]
        return total

    for peer in line_peers:
        send(own_pos, lpos.at[line_slot], pos_send, pos_recv.at[1], peer)
    for peer in plane_peers:
        send(own_pos, ppos.at[slot], pos_send, pos_recv.at[0], peer)
    for h in range(2):
        gather_start(0, b_ref, h)
    for h in range(2):
        gather_second(0, b_ref, h)
    line[0, z] = b_ref[...]
    line_step(0, 1)
    ppos[slot] = own_pos[...]
    lpos[line_slot] = own_pos[...]
    gath[0, slot] = b_ref[...]
    inv[...] = jnp.broadcast_to(1.0 / own_pos[3:4, :], (B, B)).T
    gather_spread(0)
    wait(lpos.at[0 : LINE - 1], pos_recv.at[1])

    def spread(t, _):
        for u in range(4):
            rows = pl.ds(pl.multiple_of(t * 4 * B + u * B, B), B)
            for a in range(3):
                xb[a, rows, :] = jnp.broadcast_to(lpos[t * 4 + u, a : a + 1, :], (B, B)).T
        return 0

    lax.fori_loop(0, LINE // 4, spread, 0)
    gather_forward(0, (0,))
    wait(ppos.at[0 : PLANE - 1], pos_recv.at[0])

    def evaluate(t, _):
        rows = pl.ds(pl.multiple_of(t * B, B), B)
        for j in range(PLANE):
            d0 = xb[0, rows, :] - ppos[j, 0:1, :]
            d1 = xb[1, rows, :] - ppos[j, 1:2, :]
            d2 = xb[2, rows, :] - ppos[j, 2:3, :]
            weight = lax.rsqrt(d0 * d0 + d1 * d1 + d2 * d2 + softening)
            high = weight.astype(BF16)
            khi[rows, j * B : (j + 1) * B] = high
            klo[rows, j * B : (j + 1) * B] = (weight - high.astype(F32)).astype(BF16)
        return 0

    lax.fori_loop(0, 6, evaluate, 0)
    gather_forward(0, (1, 3))
    line_step(0, 2)
    lax.fori_loop(6, 12, evaluate, 0)
    gather_forward(0, (2,))
    lax.fori_loop(12, LINE, evaluate, 0)

    def split_values(m):
        def step(s, _):
            rows = pl.ds(pl.multiple_of(s * B, B), B)
            value = gath[m, s]
            high = value.astype(BF16)
            vhi[rows, :] = high
            vlo[rows, :] = (value - high.astype(F32)).astype(BF16)
            return 0

        lax.fori_loop(0, PLANE, step, 0)

    def sub_rows(c):
        return pl.ds(c * SR, SR)

    def ring_target(way, s):
        return at_z(4 - s) if way == 0 else at_z(4 + s)

    def ring_peer(way):
        return device(x, y, at_z(1 if way == 0 else NZ - 1), k)

    def join_sibling(m, dest):
        wait(sib.at[m, dest], s_recv.at[m, dest])
        mine = pl.ds(pl.multiple_of(dest * 2 * B + k * B, B), B)
        sib[m, dest] = sib[m, dest] + part[mine, :]

    def ring_step(m, s):
        for i in range(SUB):
            for way in range(2):
                c = 2 * (i % (SUB // 2)) + (1 - way if i < SUB // 2 else way)
                if s == 0 and c % 2 != way:
                    continue
                dest = ring_target(way, s)
                if s == 0 or (s == 1 and c % 2 != way):
                    piece = sib.at[m, dest, sub_rows(c)]
                else:
                    piece = ring.at[m, way, s - 1, sub_rows(c)]
                    wait(piece, r_recv.at[m, way, s - 1, c])
                    piece[...] = piece[...] + sib[m, dest, sub_rows(c), :]
                send(piece, ring.at[m, way, s, sub_rows(c)], r_send.at[m], r_recv.at[m, way, s, c], ring_peer(way))

    def ring_result(m, c):
        for way in range(2):
            wait(ring.at[m, way, 3, sub_rows(c)], r_recv.at[m, way, 3, c])
        return sib[m, z, sub_rows(c), :] + ring[m, 0, 3, sub_rows(c), :] + ring[m, 1, 3, sub_rows(c), :]

    def products(m):
        def step(i, _):
            off = 4 + (1 - 2 * lax.rem(i, 2)) * ((i + 1) // 2)
            dest = at_z(off)
            rows = pl.ds(pl.multiple_of(dest * 2 * B, 2 * B), 2 * B)
            high = khi[rows, :]
            total = jnp.dot(klo[rows, :], vhi[...], preferred_element_type=F32)
            total = total + jnp.dot(high, vlo[...], preferred_element_type=F32)
            part[rows, :] = total + jnp.dot(high, vhi[...], preferred_element_type=F32)
            other = pl.ds(pl.multiple_of(dest * 2 * B + (1 - k) * B, B), B)
            send(part.at[other], sib.at[m, dest], s_send.at[m], s_recv.at[m, dest], sibling)

            for at, work in hooks:
                pl.when(i == at)(work)

            return 0

        def first():
            join_sibling(m, at_z(4))
            ring_step(m, 0)

        def second():
            join_sibling(m, at_z(3))
            join_sibling(m, at_z(5))
            ring_step(m, 1)

        hooks = ((1, first), (4, second)) if m == 0 else ((0, lambda: line_step(1, 4)), (1, first), (6, second))
        lax.fori_loop(0, NZ, step, 0)
        for d in (2, 6):
            join_sibling(m, at_z(d))
        if m == 0:
            ring_step(m, 2)
        for d in (1, 7, 0):
            join_sibling(m, at_z(d))

    ar_src[...] = jnp.zeros_like(ar_src)
    gather_finish(0)
    split_values(0)
    line_step(0, 3)
    products(0)
    ring_step(0, 3)
    pack(0, 0, b_ref[...] * b_ref[...])
    for h in range(2):
        for c in range(h * SUB // 2, (h + 1) * SUB // 2):
            rows = slice(c * SR, (c + 1) * SR)
            own = jnp.concatenate([inv[rows, :], inv[rows, :]], axis=1) * b_ref[rows, :]
            w1[rows, :] = own + kernel_scale * ring_result(0, c)
        gather_start(1, w1, h)
    for h in range(2):
        gather_second(1, w1, h)
    line[1, z] = w1[...]
    line_step(1, 1)
    gath[1, slot] = w1[...]
    pack(0, 1, b_ref[...] * w1[...])
    wait(gath.at[0, 0:NZ], s_send.at[0])
    gather_spread(1)
    line_step(0, 4)
    line_step(1, 2)
    sum_start(0)
    gather_forward(1, (0, 1, 3))
    line_step(1, 3)
    gather_forward(1, (2,))
    gather_finish(1)
    sum_middle(0)
    split_values(1)
    products(1)
    sums = sum_finish(0)
    norm0 = unpack(sums, 0)
    curvature = unpack(sums, 1)
    alpha = norm0 / curvature
    line_finish(0)
    line_finish(1)
    r = b_ref[...] - alpha * w1[...]
    sol_ref[...] = r
    scaled = jnp.concatenate([inv[...], inv[...]], axis=1) * w1[...]

    def meet(dest, total):
        return total + (line[0, dest] - alpha * line[1, dest]) * sib[1, dest]

    met = lax.fori_loop(0, NZ, meet, jnp.zeros((B, R), F32))
    pack(1, 0, r * r)
    pack(1, 1, r * (w1[...] - alpha * scaled) - (kernel_scale * alpha) * met)
    pack(1, 2, w1[...] * r)
    sum_start(1)
    ring_step(1, 2)
    sum_middle(1)
    ring_step(1, 3)
    res_ref[...] = w1[...] - alpha * (scaled + kernel_scale * sib[1, z])
    for c in range(SUB):
        for way in range(2):
            wait(ring.at[1, way, 3, sub_rows(c)], r_recv.at[1, way, 3, c])
    res_ref[...] = res_ref[...] - (kernel_scale * alpha) * (ring[1, 0, 3] + ring[1, 1, 3])
    sums = sum_finish(1)
    norm1 = unpack(sums, 0)
    beta = norm1 / norm0
    step_size = norm1 / (unpack(sums, 1) + 2.0 * beta * unpack(sums, 2) + beta * beta * curvature)
    r = sol_ref[...]
    sol_ref[...] = alpha * b_ref[...] + step_size * (r + beta * b_ref[...])
    res_ref[...] = r - step_size * (res_ref[...] + beta * w1[...])

    wait(gath.at[0, 0, 0 : B - 8], pos_send)
    for m in range(2):
        wait(gath.at[m, 0 : PLANE - 1], g_send.at[m])
        wait(gath.at[m, 0 : NZ - 1], r_send.at[m])
        wait(gath.at[m, 0 : NZ - 1], l_send.at[m])
    wait(gath.at[1, 0:NZ], s_send.at[1])
    for i in range(2):
        wait(ar_line.at[i, 0 : LINE - 1], ar_send.at[i, 1])


def body(positions, radii, right_side):
    total = B * lax.axis_size("row") * lax.axis_size("col")
    kernel_scale, softening = constants(total)
    vmem = pl.BlockSpec(memory_space=pltpu.VMEM)
    out = jax.ShapeDtypeStruct((B, R), F32)
    dma = pltpu.SemaphoreType.DMA
    cols = PLANE * B
    return pl.pallas_call(
        functools.partial(kernel, kernel_scale, softening),
        out_shape=(out, out),
        in_specs=[vmem] * 3,
        out_specs=(vmem, vmem),
        scratch_shapes=[
            pltpu.VMEM((LINE * B, cols), BF16),
            pltpu.VMEM((LINE * B, cols), BF16),
            pltpu.VMEM((2, PLANE, B, R), F32),
            pltpu.VMEM((cols, R), BF16),
            pltpu.VMEM((cols, R), BF16),
            pltpu.VMEM((LINE * B, R), F32),
            pltpu.VMEM((2, NZ, B, R), F32),
            pltpu.VMEM((2, 2, 4, B, R), F32),
            pltpu.VMEM((3, LINE * B, B), F32),
            pltpu.VMEM((PLANE, 8, B), F32),
            pltpu.VMEM((LINE, 8, B), F32),
            pltpu.VMEM((8, B), F32),
            pltpu.VMEM((B, B), F32),
            pltpu.VMEM((B, R), F32),
            pltpu.VMEM((2, NZ, B, R), F32),
            pltpu.VMEM((2, 8, B), F32),
            pltpu.VMEM((2, PLANE, 8, B), F32),
            pltpu.VMEM((2, LINE, 8, B), F32),
            dma,
            dma((2,)),
            dma((2,)),
            dma((2, 2, PLANE)),
            dma((2, 2, 2, NX)),
            dma((2,)),
            dma((2, NZ, 2)),
            dma((2,)),
            dma((2, NZ)),
            dma((2,)),
            dma((2, 2, 4, SUB)),
            dma((2, 2)),
            dma((2, 2)),
        ],
        compiler_params=pltpu.CompilerParams(
            collective_id=0, has_side_effects=True, vmem_limit_bytes=56 << 20
        ),
        name="cg",
    )(positions, radii.reshape(1, B), right_side)


def solution(mesh):
    return jax.shard_map(
        body,
        mesh=mesh,
        in_specs=(P(None, ("row", "col")), P(("row", "col")), P(("row", "col"), None)),
        out_specs=(P(("row", "col"), None), P(("row", "col"), None)),
        check_vma=False,
    )
```

```python
import functools

import jax
import jax.numpy as jnp
from jax import lax
from jax.experimental import pallas as pl
from jax.experimental.pallas import tpu as pltpu
from jax.sharding import PartitionSpec as P

MESH = pl.DeviceIdType.MESH
B = 128
R = 256
NX, NY, NZ = 4, 4, 8
PLANE = NX * NY
LINE = NZ * 2
HALF = B // 2
SUB = 4
SR = B // SUB
F32 = jnp.float32
BF16 = jnp.bfloat16


def constants(total):
    kernel_scale = float(total) ** (-0.5)
    spacing = 0.25 * float(total) ** (-1.0 / 3.0)
    return (kernel_scale, spacing * spacing)


def kernel(
    kernel_scale, softening,
    pos_ref, rad_ref, b_ref, sol_ref, res_ref,
    khi, klo, gath, vhi, vlo, part, sib, ring, xb, ppos, lpos, own_pos, inv, w1, line, ar_src, ar_plane, ar_line,
    pos_send, pos_recv, g_send, g_recv, q_recv, l_send, l_recv, s_send, s_recv, r_send, r_recv, ar_send, ar_recv,
):
    row, col = lax.axis_index("row"), lax.axis_index("col")
    x, y = col // 4, lax.rem(row, 4)
    z, k = (row // 4) * 2 + lax.rem(col // 2, 2), lax.rem(col, 2)

    def device(xx, yy, zz, kk):
        return {"row": (zz // 2) * 4 + yy, "col": xx * 4 + lax.rem(zz, 2) * 2 + kk}

    def at_x(d):
        return lax.rem(x + d, NX)

    def at_y(d):
        return lax.rem(y + d, NY)

    def at_z(d):
        return lax.rem(z + d, NZ)

    def send(src, dst, ssem, rsem, dev):
        pltpu.make_async_remote_copy(
            src_ref=src, dst_ref=dst, send_sem=ssem, recv_sem=rsem, device_id=dev, device_id_type=MESH
        ).start()

    def wait(ref, sem):
        pltpu.make_async_copy(ref, ref, sem).wait()

    plane_peers = [device(at_x(dx), at_y(dy), z, k) for dx in range(NX) for dy in range(NY) if dx or dy]
    line_peers = [
        device(x, y, at_z(dz), lax.rem(k + dk, 2)) for dz in range(NZ) for dk in range(2) if dz or dk
    ]
    sibling = device(x, y, z, 1 - k)
    slot = x * NY + y
    line_slot = z * 2 + k

    barrier = pltpu.get_barrier_semaphore()
    for peer in plane_peers + line_peers:
        pl.semaphore_signal(barrier, 1, device_id=peer, device_id_type=MESH)
    own_pos[...] = jnp.zeros_like(own_pos)
    own_pos[0:3, :] = pos_ref[...]
    own_pos[3:4, :] = rad_ref[...]
    pl.semaphore_wait(barrier, len(plane_peers) + len(line_peers))

    def half_rows(h):
        return pl.ds(h * HALF, HALF)

    def plane_slot(h, first, second):
        return at_x(first) * NY + at_y(second) if h == 0 else at_x(second) * NY + at_y(first)

    def first_peer(h, d):
        return device(at_x(d), y, z, k) if h == 0 else device(x, at_y(d), z, k)

    def second_peer(h, d):
        return device(x, at_y(d), z, k) if h == 0 else device(at_x(d), y, z, k)

    def first_at(h, d):
        return at_x(d) if h == 0 else at_y(d)

    def gather_start(m, src, h):
        for d in (1, 3, 2):
            send(src.at[half_rows(h)], gath.at[m, slot, half_rows(h)], g_send.at[m], g_recv.at[m, h, slot], first_peer(h, d))

    def gather_second(m, src, h):
        for d in (1, 3):
            send(src.at[half_rows(h)], gath.at[m, slot, half_rows(h)], g_send.at[m], g_recv.at[m, h, slot], second_peer(h, d))

    def gather_spread(m):
        for o in (1, 3, 2):
            for h in range(2):
                s = plane_slot(h, o, 0)
                piece = gath.at[m, s, half_rows(h)]
                wait(piece, g_recv.at[m, h, s])
                for d in (1, 3):
                    send(piece, piece, g_send.at[m], g_recv.at[m, h, s], second_peer(h, d))

    def quarter(m, h, s, q):
        return gath.at[m, s, pl.ds(h * HALF + q * HALF // 2, HALF // 2)]

    def gather_forward(m, offsets):
        for o in offsets:
            for h in range(2):
                for q in range(2):
                    s = plane_slot(h, o, 3 if q == 0 else 1)
                    wait(gath.at[m, s, half_rows(h)], g_recv.at[m, h, s])
                    piece = quarter(m, h, s, q)
                    send(piece, piece, g_send.at[m], q_recv.at[m, h, q, first_at(h, o)], second_peer(h, 1 if q == 0 else 3))

    def gather_finish(m):
        for o in (0, 1, 3, 2):
            for h in range(2):
                for q in range(2):
                    wait(quarter(m, h, plane_slot(h, o, 2), q), q_recv.at[m, h, q, first_at(h, o)])

    def line_step(m, j):
        for p in range(2):
            for way in range(2):
                if j == 4 and p != way:
                    continue
                source = at_z(1 - j + NZ if way == 0 else j - 1)
                piece = line.at[m, source, half_rows(p)]
                if j > 1:
                    wait(piece, l_recv.at[m, source, p])
                peer = device(x, y, at_z(1 if way == 0 else NZ - 1), k)
                send(piece, piece, l_send.at[m], l_recv.at[m, source, p], peer)

    def line_finish(m):
        wait(line.at[m, at_z(5), half_rows(1)], l_recv.at[m, at_z(5), 1])
        wait(line.at[m, at_z(3), half_rows(0)], l_recv.at[m, at_z(3), 0])
        for p in range(2):
            wait(line.at[m, at_z(4), half_rows(p)], l_recv.at[m, at_z(4), p])

    def pack(i, j, term):
        column = jnp.sum(term, axis=0, keepdims=True)
        ar_src[i, 2 * j : 2 * j + 1, :] = column[:, :B]
        ar_src[i, 2 * j + 1 : 2 * j + 2, :] = column[:, B:]

    def unpack(total, j):
        return jnp.concatenate([total[2 * j : 2 * j + 1, :], total[2 * j + 1 : 2 * j + 2, :]], axis=1)

    def sum_start(i):
        ar_plane[i, slot] = ar_src[i]
        for peer in plane_peers:
            send(ar_src.at[i], ar_plane.at[i, slot], ar_send.at[i, 0], ar_recv.at[i, 0], peer)

    def sum_middle(i):
        wait(ar_plane.at[i, 0 : PLANE - 1], ar_send.at[i, 0])
        wait(ar_plane.at[i, 0 : PLANE - 1], ar_recv.at[i, 0])
        total = ar_plane[i, 0]
        for s in range(1, PLANE):
            total = total + ar_plane[i, s]
        ar_src[i] = total
        ar_line[i, line_slot] = total
        for peer in line_peers:
            send(ar_src.at[i], ar_line.at[i, line_slot], ar_send.at[i, 1], ar_recv.at[i, 1], peer)

    def sum_finish(i):
        wait(ar_line.at[i, 0 : LINE - 1], ar_recv.at[i, 1])
        total = ar_line[i, 0]
        for s in range(1, LINE):
            total = total + ar_line[i, s]
        return total

    for peer in line_peers:
        send(own_pos, lpos.at[line_slot], pos_send, pos_recv.at[1], peer)
    for peer in plane_peers:
        send(own_pos, ppos.at[slot], pos_send, pos_recv.at[0], peer)
    for h in range(2):
        gather_start(0, b_ref, h)
    for h in range(2):
        gather_second(0, b_ref, h)
    line[0, z] = b_ref[...]
    line_step(0, 1)
    ppos[slot] = own_pos[...]
    lpos[line_slot] = own_pos[...]
    gath[0, slot] = b_ref[...]
    inv[...] = jnp.broadcast_to(1.0 / own_pos[3:4, :], (B, B)).T
    gather_spread(0)
    wait(lpos.at[0 : LINE - 1], pos_recv.at[1])

    def spread(t, _):
        for u in range(4):
            rows = pl.ds(pl.multiple_of(t * 4 * B + u * B, B), B)
            for a in range(3):
                xb[a, rows, :] = jnp.broadcast_to(lpos[t * 4 + u, a : a + 1, :], (B, B)).T
        return 0

    lax.fori_loop(0, LINE // 4, spread, 0)
    gather_forward(0, (0,))
    wait(ppos.at[0 : PLANE - 1], pos_recv.at[0])

    def evaluate(t, _):
        rows = pl.ds(pl.multiple_of(t * B, B), B)
        for j in range(PLANE):
            d0 = xb[0, rows, :] - ppos[j, 0:1, :]
            d1 = xb[1, rows, :] - ppos[j, 1:2, :]
            d2 = xb[2, rows, :] - ppos[j, 2:3, :]
            weight = lax.rsqrt(d0 * d0 + d1 * d1 + d2 * d2 + softening)
            high = weight.astype(BF16)
            khi[rows, j * B : (j + 1) * B] = high
            klo[rows, j * B : (j + 1) * B] = (weight - high.astype(F32)).astype(BF16)
        return 0

    lax.fori_loop(0, 6, evaluate, 0)
    gather_forward(0, (1, 3))
    line_step(0, 2)
    lax.fori_loop(6, 12, evaluate, 0)
    gather_forward(0, (2,))
    lax.fori_loop(12, LINE, evaluate, 0)

    def split_values(m):
        def step(s, _):
            rows = pl.ds(pl.multiple_of(s * B, B), B)
            value = gath[m, s]
            high = value.astype(BF16)
            vhi[rows, :] = high
            vlo[rows, :] = (value - high.astype(F32)).astype(BF16)
            return 0

        lax.fori_loop(0, PLANE, step, 0)

    def sub_rows(c):
        return pl.ds(c * SR, SR)

    def ring_target(way, s):
        return at_z(4 - s) if way == 0 else at_z(4 + s)

    def ring_peer(way):
        return device(x, y, at_z(1 if way == 0 else NZ - 1), k)

    def join_sibling(m, dest):
        wait(sib.at[m, dest], s_recv.at[m, dest])
        mine = pl.ds(pl.multiple_of(dest * 2 * B + k * B, B), B)
        sib[m, dest] = sib[m, dest] + part[mine, :]

    def ring_step(m, s):
        for i in range(SUB):
            for way in range(2):
                c = 2 * (i % (SUB // 2)) + (1 - way if i < SUB // 2 else way)
                if s == 0 and c % 2 != way:
                    continue
                dest = ring_target(way, s)
                if s == 0 or (s == 1 and c % 2 != way):
                    piece = sib.at[m, dest, sub_rows(c)]
                else:
                    piece = ring.at[m, way, s - 1, sub_rows(c)]
                    wait(piece, r_recv.at[m, way, s - 1, c])
                    piece[...] = piece[...] + sib[m, dest, sub_rows(c), :]
                send(piece, ring.at[m, way, s, sub_rows(c)], r_send.at[m], r_recv.at[m, way, s, c], ring_peer(way))

    def ring_result(m, c):
        for way in range(2):
            wait(ring.at[m, way, 3, sub_rows(c)], r_recv.at[m, way, 3, c])
        return sib[m, z, sub_rows(c), :] + ring[m, 0, 3, sub_rows(c), :] + ring[m, 1, 3, sub_rows(c), :]

    def products(m):
        def step(i, _):
            off = 4 + (1 - 2 * lax.rem(i, 2)) * ((i + 1) // 2)
            dest = at_z(off)
            rows = pl.ds(pl.multiple_of(dest * 2 * B, 2 * B), 2 * B)
            high = khi[rows, :]
            total = jnp.dot(klo[rows, :], vhi[...], preferred_element_type=F32)
            total = total + jnp.dot(high, vlo[...], preferred_element_type=F32)
            part[rows, :] = total + jnp.dot(high, vhi[...], preferred_element_type=F32)
            other = pl.ds(pl.multiple_of(dest * 2 * B + (1 - k) * B, B), B)
            send(part.at[other], sib.at[m, dest], s_send.at[m], s_recv.at[m, dest], sibling)

            for at, work in hooks:
                pl.when(i == at)(work)

            return 0

        def first():
            join_sibling(m, at_z(4))
            ring_step(m, 0)

        def second():
            join_sibling(m, at_z(3))
            join_sibling(m, at_z(5))
            ring_step(m, 1)

        hooks = ((1, first), (4, second)) if m == 0 else ((1, first), (3, lambda: line_step(1, 4)), (6, second))
        lax.fori_loop(0, NZ, step, 0)
        for d in (2, 6):
            join_sibling(m, at_z(d))
        if m == 0:
            ring_step(m, 2)
        for d in (1, 7, 0):
            join_sibling(m, at_z(d))

    ar_src[...] = jnp.zeros_like(ar_src)
    gather_finish(0)
    split_values(0)
    line_step(0, 3)
    products(0)
    ring_step(0, 3)
    pack(0, 0, b_ref[...] * b_ref[...])
    for h in range(2):
        for c in range(h * SUB // 2, (h + 1) * SUB // 2):
            rows = slice(c * SR, (c + 1) * SR)
            own = jnp.concatenate([inv[rows, :], inv[rows, :]], axis=1) * b_ref[rows, :]
            w1[rows, :] = own + kernel_scale * ring_result(0, c)
        gather_start(1, w1, h)
    for h in range(2):
        gather_second(1, w1, h)
    line[1, z] = w1[...]
    line_step(1, 1)
    gath[1, slot] = w1[...]
    pack(0, 1, b_ref[...] * w1[...])
    wait(gath.at[0, 0:NZ], s_send.at[0])
    gather_spread(1)
    line_step(0, 4)
    line_step(1, 2)
    sum_start(0)
    gather_forward(1, (0, 1, 3))
    gather_forward(1, (2,))
    sum_middle(0)
    gather_finish(1)
    line_step(1, 3)
    split_values(1)
    products(1)
    sums = sum_finish(0)
    norm0 = unpack(sums, 0)
    curvature = unpack(sums, 1)
    alpha = norm0 / curvature
    line_finish(0)
    line_finish(1)
    r = b_ref[...] - alpha * w1[...]
    sol_ref[...] = r
    scaled = jnp.concatenate([inv[...], inv[...]], axis=1) * w1[...]

    def meet(dest, total):
        return total + (line[0, dest] - alpha * line[1, dest]) * sib[1, dest]

    met = lax.fori_loop(0, NZ, meet, jnp.zeros((B, R), F32))
    pack(1, 0, r * r)
    pack(1, 1, r * (w1[...] - alpha * scaled) - (kernel_scale * alpha) * met)
    pack(1, 2, w1[...] * r)
    sum_start(1)
    ring_step(1, 2)
    sum_middle(1)
    ring_step(1, 3)
    res_ref[...] = w1[...] - alpha * (scaled + kernel_scale * sib[1, z])
    for c in range(SUB):
        for way in range(2):
            wait(ring.at[1, way, 3, sub_rows(c)], r_recv.at[1, way, 3, c])
    res_ref[...] = res_ref[...] - (kernel_scale * alpha) * (ring[1, 0, 3] + ring[1, 1, 3])
    sums = sum_finish(1)
    norm1 = unpack(sums, 0)
    beta = norm1 / norm0
    step_size = norm1 / (unpack(sums, 1) + 2.0 * beta * unpack(sums, 2) + beta * beta * curvature)
    r = sol_ref[...]
    sol_ref[...] = alpha * b_ref[...] + step_size * (r + beta * b_ref[...])
    res_ref[...] = r - step_size * (res_ref[...] + beta * w1[...])

    wait(gath.at[0, 0, 0 : B - 8], pos_send)
    for m in range(2):
        wait(gath.at[m, 0 : PLANE - 1], g_send.at[m])
        wait(gath.at[m, 0 : NZ - 1], r_send.at[m])
        wait(gath.at[m, 0 : NZ - 1], l_send.at[m])
    wait(gath.at[1, 0:NZ], s_send.at[1])
    for i in range(2):
        wait(ar_line.at[i, 0 : LINE - 1], ar_send.at[i, 1])


def body(positions, radii, right_side):
    total = B * lax.axis_size("row") * lax.axis_size("col")
    kernel_scale, softening = constants(total)
    vmem = pl.BlockSpec(memory_space=pltpu.VMEM)
    out = jax.ShapeDtypeStruct((B, R), F32)
    dma = pltpu.SemaphoreType.DMA
    cols = PLANE * B
    return pl.pallas_call(
        functools.partial(kernel, kernel_scale, softening),
        out_shape=(out, out),
        in_specs=[vmem] * 3,
        out_specs=(vmem, vmem),
        scratch_shapes=[
            pltpu.VMEM((LINE * B, cols), BF16),
            pltpu.VMEM((LINE * B, cols), BF16),
            pltpu.VMEM((2, PLANE, B, R), F32),
            pltpu.VMEM((cols, R), BF16),
            pltpu.VMEM((cols, R), BF16),
            pltpu.VMEM((LINE * B, R), F32),
            pltpu.VMEM((2, NZ, B, R), F32),
            pltpu.VMEM((2, 2, 4, B, R), F32),
            pltpu.VMEM((3, LINE * B, B), F32),
            pltpu.VMEM((PLANE, 8, B), F32),
            pltpu.VMEM((LINE, 8, B), F32),
            pltpu.VMEM((8, B), F32),
            pltpu.VMEM((B, B), F32),
            pltpu.VMEM((B, R), F32),
            pltpu.VMEM((2, NZ, B, R), F32),
            pltpu.VMEM((2, 8, B), F32),
            pltpu.VMEM((2, PLANE, 8, B), F32),
            pltpu.VMEM((2, LINE, 8, B), F32),
            dma,
            dma((2,)),
            dma((2,)),
            dma((2, 2, PLANE)),
            dma((2, 2, 2, NX)),
            dma((2,)),
            dma((2, NZ, 2)),
            dma((2,)),
            dma((2, NZ)),
            dma((2,)),
            dma((2, 2, 4, SUB)),
            dma((2, 2)),
            dma((2, 2)),
        ],
        compiler_params=pltpu.CompilerParams(
            collective_id=0, has_side_effects=True, vmem_limit_bytes=56 << 20
        ),
        name="cg",
    )(positions, radii.reshape(1, B), right_side)


def solution(mesh):
    return jax.shard_map(
        body,
        mesh=mesh,
        in_specs=(P(None, ("row", "col")), P(("row", "col")), P(("row", "col"), None)),
        out_specs=(P(("row", "col"), None), P(("row", "col"), None)),
        check_vma=False,
    )
```
